256 devices in a mesh: region: 32 (over z, x), shard: 8 (over y, core).
Axes of the slice: x: 4, y: 4, z: 8, core: 2. Of those that a mesh axis runs over, the one named last changes fastest.
Arguments:
- grid_rows: bfloat16 [262144, 1024], P(('region', 'shard')), may hold values from -6 to 6
- node_inputs: bfloat16 [65536, 1024], P(('region', 'shard')), may hold values from -6 to 6
- row_weight: bfloat16 [1024, 512], replicated, may hold values from -0.1875 to 0.1875
- node_weight: bfloat16 [1024, 512], replicated, may hold values from -0.1875 to 0.1875
- edge_bias: float32 [512], replicated, may hold values from -3 to 3
- edge_out_weight: bfloat16 [512, 1024], replicated, may hold values from -0.125 to 0.125
- norm_gain: float32 [1024], replicated, may hold values from 0.5 to 1.5
- attn_weight: bfloat16 [1024, 3072], replicated
- attn_out_weight: bfloat16 [1024, 1024], replicated, may hold values from -0.1875 to 0.1875
- edge_source: int32 [4096, 128], P(('region', 'shard')), may hold values from 0 to 1023
- edge_target: int32 [4096, 128], P(('region', 'shard')), may hold values from 0 to 255
- block_count: int32 [256], P(('region', 'shard')), may hold values from 1 to 16, as said below
Outputs:
- mixed: bfloat16 [65536, 1024], P(('region', 'shard'))
The draws below stay inside these ranges and needn't reach their ends.
Inputs may be any that keep to these rules, and one draw needn't show every extreme that they name: `block_count`: some tile uses all 16 blocks. `edge_source`: blocks at or after a tile's block_count are never read.
All inputs are finite; a program needn't handle non-finite values.
Results may differ from the reference program's by a relative error of at most 0.0061.
Values may be sent and summed in bfloat16 or wider, within the bound.
A program may use at most 64 MiB of HBM per device.

```python
import jax
import jax.numpy as jnp
from jax import lax

D = 1024
HEADS = 16
EH = 512
WINDOW = 1120
EB = 128
NODE_SH = 256
SEND = 32
NB = 16
GRID_DEV = 1024
GRID = 262144
NODES = 65536
N_REGION = 32
N_SHARD = 8
DEVICES = 256


def draw_attn_weight(key, part):
    first = jax.random.fold_in(jax.random.fold_in(key, 17), 0)
    base = jax.random.normal(first, (D, 3 * D), jnp.float32) / jnp.sqrt(jnp.float32(D))
    return base.astype(jnp.bfloat16)


def draw_block_count(key, part):
    first, second, third = jax.random.split(jax.random.fold_in(key, 29), 3)
    base = jax.random.randint(first, (DEVICES,), 1, NB // 2 + 1)
    chosen = jax.random.randint(second, (DEVICES,), 0, 8) == 0
    single = jax.random.randint(third, (), 0, DEVICES)
    chosen = chosen | (jnp.arange(DEVICES) == single)
    return jnp.where(chosen, NB, base).astype(jnp.int32)


def set_ends(values, rng, smallest, top_value):
    dims = values.shape
    spot = [jax.random.randint(jax.random.fold_in(rng, axis), (), 0, dims[axis]) for axis in range(len(dims))]
    values = values.at[tuple(spot)].set(smallest)
    longest = dims.index(max(dims))
    spot[longest] = (spot[longest] + 1) % dims[longest]
    return values.at[tuple(spot)].set(top_value)


def shard_levels(stream_key, dims, cuts, smallest, high):
    level, own = 1.0, jax.random.fold_in(stream_key, 6)
    for dim, parts in cuts:
        heights = jnp.exp(jax.random.uniform(jax.random.fold_in(own, dim), (parts,), jnp.float32, smallest / len(cuts), high / len(cuts)))
        level = level * jnp.repeat(heights, dims[dim] // parts).reshape([-1 if axis == dim else 1 for axis in range(len(dims))])
    return level


def scatter_about(rng, shape, deviation, reach, cuts=(), held_as=jnp.bfloat16):
    loudness = shard_levels(rng, shape, cuts, -0.22, 0.18) if cuts else 1.0
    array = jax.random.normal(rng, shape, jnp.float32) * deviation * loudness
    return jnp.minimum(jnp.maximum(array, -reach), reach).astype(held_as)


def setup_inputs(seed: int = 0) -> dict:
    splits = jax.random.split(jax.random.key(seed), 13)
    return {
        "grid_rows": scatter_about(splits[0], (GRID, D), 1.0, 6.0, ((0, 256),)),
        "node_inputs": scatter_about(splits[1], (NODES, D), 1.0, 6.0, ((0, 256),)),
        "row_weight": scatter_about(splits[2], (D, EH), D ** -0.5, 0.1875),
        "node_weight": scatter_about(splits[3], (D, EH), D ** -0.5, 0.1875),
        "edge_bias": scatter_about(splits[4], (EH,), 0.5, 3.0, (), jnp.float32),
        "edge_out_weight": scatter_about(splits[5], (EH, D), (4 * EH) ** -0.5, 0.125),
        "norm_gain": jnp.clip(1.0 + 0.1 * jax.random.normal(splits[6], (D,), jnp.float32), 0.5, 1.5),
        "attn_weight": draw_attn_weight(jax.random.fold_in(splits[12], 71), 0),
        "attn_out_weight": scatter_about(splits[8], (D, D), D ** -0.5, 0.1875),
        "edge_source": set_ends(jax.random.randint(splits[9], (DEVICES * NB, EB), 0, GRID_DEV), jax.random.fold_in(splits[9], 1), 0, GRID_DEV - 1).astype(jnp.int32),
        "edge_target": set_ends(jax.random.randint(splits[10], (DEVICES * NB, EB), 0, NODE_SH), jax.random.fold_in(splits[10], 1), 0, NODE_SH - 1).astype(jnp.int32),
        "block_count": draw_block_count(jax.random.fold_in(splits[12], 71), 0),
    }


def reference(grid_rows, node_inputs, row_weight, node_weight, edge_bias, edge_out_weight, norm_gain, attn_weight, attn_out_weight, edge_source, edge_target, block_count):
    regions = N_REGION
    shards = N_SHARD
    tiles = regions * shards
    projected = jnp.dot(grid_rows, row_weight, preferred_element_type=jnp.float32).astype(jnp.bfloat16)
    node_terms = (jnp.dot(node_inputs, node_weight, preferred_element_type=jnp.float32) + edge_bias.astype(jnp.float32)).astype(jnp.bfloat16)
    arrived = projected.reshape(regions, shards, regions, SEND, EH).transpose(2, 1, 0, 3, 4).reshape(tiles, GRID_DEV, EH)
    sources = edge_source.reshape(tiles, NB, EB)
    targets = edge_target.reshape(tiles, NB, EB)
    terms = node_terms.reshape(tiles, NODE_SH, EH)
    inputs = node_inputs.reshape(tiles, NODE_SH, D)

    def one_tile(packed):
        rows_in, src_tile, tgt_tile, term_tile, input_tile, used = packed

        def add_block(index, running):
            target = tgt_tile[index]
            picked = jnp.take(rows_in, src_tile[index], axis=0).astype(jnp.float32)
            preact = picked + jnp.take(term_tile, target, axis=0).astype(jnp.float32)
            hidden = jax.nn.silu(preact).astype(jnp.bfloat16)
            message = jnp.dot(hidden, edge_out_weight, preferred_element_type=jnp.float32).astype(jnp.bfloat16)
            return running + jax.ops.segment_sum(message.astype(jnp.float32), target, num_segments=NODE_SH)
        summed = lax.fori_loop(0, used, add_block, input_tile.astype(jnp.float32))
        return summed.astype(jnp.bfloat16)
    node_state = lax.map(one_tile, (arrived, sources, targets, terms, inputs, block_count)).reshape(tiles * NODE_SH, D)
    values_in = node_state.astype(jnp.float32)
    average = lax.optimization_barrier(jnp.mean(values_in, axis=1, keepdims=True))
    centred = values_in - average
    spread = lax.optimization_barrier(jnp.mean(centred * centred, axis=1, keepdims=True))
    normed = (centred * lax.rsqrt(spread + 1e-05) * norm_gain.astype(jnp.float32)).astype(jnp.bfloat16)
    projections = jnp.dot(normed, attn_weight, preferred_element_type=jnp.float32).astype(jnp.bfloat16)
    count_nodes = tiles * NODE_SH
    half_win = WINDOW // 2
    head_size = D // HEADS
    queries = projections[:, :D].reshape(count_nodes, HEADS, head_size)
    key_rows = jnp.pad(projections[:, D:2 * D].reshape(count_nodes, HEADS, head_size), ((half_win, half_win), (0, 0), (0, 0)))
    value_rows = jnp.pad(projections[:, 2 * D:].reshape(count_nodes, HEADS, head_size), ((half_win, half_win), (0, 0), (0, 0)))
    query_block = min(512, NODE_SH * N_SHARD)
    scale = 1.0 / head_size ** 0.5

    def attend(block_index):
        offset = block_index * query_block
        query_part = lax.dynamic_slice_in_dim(queries, offset, query_block, 0).astype(jnp.float32)
        key_part = lax.dynamic_slice_in_dim(key_rows, offset, query_block + 2 * half_win, 0).astype(jnp.float32)
        value_part = lax.dynamic_slice_in_dim(value_rows, offset, query_block + 2 * half_win, 0).astype(jnp.float32)
        scores = jnp.einsum('qhd,khd->hqk', query_part, key_part) * scale
        row_pos = jnp.arange(query_block)[:, None]
        col_pos = jnp.arange(query_block + 2 * half_win)[None, :]
        key_pos = offset - half_win + col_pos
        allowed = (col_pos >= row_pos) & (col_pos < row_pos + 2 * half_win) & (key_pos >= 0) & (key_pos < count_nodes)
        scores = jnp.where(allowed[None], scores, -1e+30)
        largest = lax.optimization_barrier(jnp.max(scores, axis=2, keepdims=True))
        raised = jnp.exp(scores - largest)
        weights = (raised / lax.optimization_barrier(jnp.sum(raised, axis=2, keepdims=True))).astype(jnp.bfloat16)
        result = jnp.einsum('hqk,khd->qhd', weights.astype(jnp.float32), value_part)
        return result.astype(jnp.bfloat16).reshape(query_block, D)
    attended = lax.map(attend, jnp.arange(count_nodes // query_block)).reshape(count_nodes, D)
    mixed = (values_in + jnp.dot(attended, attn_out_weight, preferred_element_type=jnp.float32)).astype(jnp.bfloat16)
    return mixed
```

```python
import jax
import jax.numpy as jnp
from jax import lax
from jax.experimental import pallas as pl
from jax.experimental.pallas import tpu as pltpu
from jax.sharding import PartitionSpec as P

HALF = 560
KEYS = 1408
CHUNKS = (
    (560, 256, 0),
    (304, 256, -1),
    (816, 256, 1),
    (48, 256, -2),
    (1072, 256, 2),
    (0, 48, -3),
    (1328, 80, 3),
)
LOG2E = 1.4426950408889634
F32 = jnp.float32
BF16 = jnp.bfloat16


def edge_kernel(count_ref, arrived, nodes, node_weight, bias, source, target, out, table, hidden, picks):
    blocks, width = source.shape
    rows = arrived.shape[0]
    tile = nodes.shape[0]
    used = count_ref[0]
    table[pl.ds(0, rows), :] = arrived[...]
    table[pl.ds(rows, tile), :] = (
        jnp.dot(nodes[...], node_weight[...], preferred_element_type=F32) + bias[...]
    ).astype(BF16)
    source_cols = jnp.transpose(source[...])
    target_cols = jnp.transpose(target[...])
    lane_rows = lax.broadcasted_iota(jnp.int32, (width, rows), 1)
    lane_tile = lax.broadcasted_iota(jnp.int32, (width, tile), 1)
    sub_tile = lax.broadcasted_iota(jnp.int32, (tile, width), 0)
    for block in range(blocks):
        span = pl.ds(block * width, width)
        onehot = jnp.concatenate(
            [
                (source_cols[:, block : block + 1] == lane_rows).astype(F32).astype(BF16),
                (target_cols[:, block : block + 1] == lane_tile).astype(F32).astype(BF16),
            ],
            axis=1,
        )
        pre = jnp.dot(onehot, table[...], preferred_element_type=F32)
        hidden[span, :] = (0.5 * pre * (1.0 + jnp.tanh(0.5 * pre))).astype(BF16)
        goal = jnp.where(block < used, target[block : block + 1, :], -1)
        picks[:, span] = (goal == sub_tile).astype(F32).astype(BF16)
    out[...] = jnp.dot(picks[...], hidden[...], preferred_element_type=F32).astype(BF16)


def window_kernel(sums, nodes, edge_out, gain, attn_weight, out_weight, mixed, queries, keys, values, attended, state):
    tile, width = mixed.shape
    own = CHUNKS[0][0]
    tiles = lax.axis_size("region") * lax.axis_size("shard")
    me = lax.axis_index("region") * lax.axis_size("shard") + lax.axis_index("shard")
    for first, rows, away in CHUNKS:
        span = pl.ds(first, rows)
        summed, embedded = sums[span, :], nodes[span, :]
        there = (me + away >= 0) & (me + away < tiles)
        if away:
            summed = jnp.where(there, summed, sums[pl.ds(own, rows), :])
            embedded = jnp.where(there, embedded, nodes[pl.ds(own, rows), :])
        held = (
            embedded.astype(F32) + jnp.dot(summed, edge_out[...], preferred_element_type=F32)
        ).astype(BF16)
        if not away:
            state[...] = held
        held = held.astype(F32)
        centred = held - jnp.mean(held, axis=1, keepdims=True)
        spread = jnp.mean(centred * centred, axis=1, keepdims=True)
        normed = (centred * lax.rsqrt(spread + 1e-05) * gain[...]).astype(BF16)
        keys[span, :] = jnp.dot(
            normed, attn_weight[:, width : 2 * width], preferred_element_type=F32
        ).astype(BF16)
        value = jnp.dot(normed, attn_weight[:, 2 * width :], preferred_element_type=F32)
        flag = there.astype(F32) if away else 1.0
        values[span, :] = (value * flag).astype(BF16)
        if not away:
            queries[...] = (
                jnp.dot(normed, attn_weight[:, :width], preferred_element_type=F32)
                * (LOG2E * 0.125)
            ).astype(BF16)
    spot = lax.broadcasted_iota(jnp.int32, (KEYS, 128), 0) - own + me * tile
    live = ((spot >= 0) & (spot < tiles * tile)).astype(F32).astype(BF16)
    lanes = lax.broadcasted_iota(jnp.int32, (tile, 128), 1)
    left_row = lax.broadcasted_iota(jnp.int32, (2 * tile, 256), 0) % tile
    left_key = lax.broadcasted_iota(jnp.int32, (2 * tile, 256), 1)
    right_row = lax.broadcasted_iota(jnp.int32, (2 * tile, KEYS - 1024), 0) % tile
    right_key = lax.broadcasted_iota(jnp.int32, (2 * tile, KEYS - 1024), 1) + 1024

    def pair(index, carry):
        span = pl.ds(pl.multiple_of(index * 128, 128), 128)
        query = queries[:, span]
        zero = jnp.zeros_like(query)
        query = jnp.concatenate(
            [jnp.where(lanes < 64, query, zero), jnp.where(lanes >= 64, query, zero)], axis=0
        )
        scores = lax.dot_general(
            query, keys[:, span], (((1,), (1,)), ((), ())), preferred_element_type=F32
        )
        scores = jnp.concatenate(
            [
                jnp.where(left_key >= left_row, scores[:, :256], -1e30),
                scores[:, 256:1024],
                jnp.where(right_key < right_row + 2 * HALF, scores[:, 1024:], -1e30),
            ],
            axis=1,
        )
        raised = jnp.exp2(scores - jnp.max(scores, axis=1, keepdims=True)).astype(BF16)
        both = jnp.dot(
            raised, jnp.concatenate([values[:, span], live], axis=1), preferred_element_type=F32
        )
        both = both[:, :128] / both[:, 128:]
        attended[:, span] = jnp.where(lanes < 64, both[:tile], both[tile:]).astype(BF16)
        return carry

    lax.fori_loop(0, width // 128, pair, 0)
    mixed[...] = (
        state[...].astype(F32)
        + jnp.dot(attended[...], out_weight[...], preferred_element_type=F32)
    ).astype(BF16)


def in_vmem(count):
    return [pl.BlockSpec(memory_space=pltpu.VMEM)] * count


def extend(own):
    tiles = lax.axis_size("region") * lax.axis_size("shard")
    pieces = {0: own}
    for _, rows, away in CHUNKS[1:]:
        part = own if rows == own.shape[0] else (own[-rows:] if away < 0 else own[:rows])
        routes = [(i, i - away) for i in range(tiles) if 0 <= i - away < tiles]
        pieces[away] = lax.ppermute(part, ("region", "shard"), routes)
    return jnp.concatenate([pieces[away] for away in sorted(pieces)], axis=0)


def local(
    grid_rows,
    node_inputs,
    row_weight,
    node_weight,
    edge_bias,
    edge_out_weight,
    norm_gain,
    attn_weight,
    attn_out_weight,
    edge_source,
    edge_target,
    block_count,
):
    tile, width = node_inputs.shape
    rows = grid_rows.shape[0]
    hidden = row_weight.shape[1]
    edges = edge_source.shape[0] * edge_source.shape[1]
    projected = jnp.dot(grid_rows, row_weight, preferred_element_type=F32).astype(BF16)
    arrived = lax.all_to_all(projected, "region", split_axis=0, concat_axis=0, tiled=True)
    all_nodes = extend(node_inputs)
    sums = pl.pallas_call(
        edge_kernel,
        out_shape=jax.ShapeDtypeStruct((tile, hidden), BF16),
        in_specs=[pl.BlockSpec(memory_space=pltpu.SMEM)] + in_vmem(6),
        out_specs=in_vmem(1)[0],
        scratch_shapes=[
            pltpu.VMEM((rows + tile, hidden), BF16),
            pltpu.VMEM((edges, hidden), BF16),
            pltpu.VMEM((tile, edges), BF16),
        ],
        name="edges",
    )(block_count, arrived, node_inputs, node_weight, edge_bias[None], edge_source, edge_target)
    all_sums = extend(sums)
    return pl.pallas_call(
        window_kernel,
        out_shape=jax.ShapeDtypeStruct((tile, width), BF16),
        in_specs=in_vmem(6),
        out_specs=in_vmem(1)[0],
        scratch_shapes=[
            pltpu.VMEM((tile, width), BF16),
            pltpu.VMEM((KEYS, width), BF16),
            pltpu.VMEM((KEYS, width), BF16),
            pltpu.VMEM((tile, width), BF16),
            pltpu.VMEM((tile, width), BF16),
        ],
        name="window",
    )(all_sums, all_nodes, edge_out_weight, norm_gain[None], attn_weight, attn_out_weight)


def solution(mesh):
    placed = (
        P(("region", "shard"), None),
        P(("region", "shard"), None),
        P(),
        P(),
        P(),
        P(),
        P(),
        P(),
        P(),
        P(("region", "shard"), None),
        P(("region", "shard"), None),
        P(("region", "shard")),
    )
    return jax.shard_map(
        local, mesh=mesh, in_specs=placed, out_specs=P(("region", "shard"), None), check_vma=False
    )
```

```python
import functools

import jax
import jax.numpy as jnp
from jax import lax
from jax.experimental import pallas as pl
from jax.experimental.pallas import tpu as pltpu
from jax.sharding import PartitionSpec as P

HALF = 560
KEYS = 1408
OWN = 560
CHUNKS = (
    (304, 256, -1),
    (816, 256, 1),
    (48, 256, -2),
    (1072, 256, 2),
    (0, 48, -3),
    (1328, 80, 3),
)
SENDS = {
    1: (304, 0, 256),
    -1: (816, 0, 256),
    2: (48, 0, 256),
    -2: (1072, 0, 256),
    3: (0, 208, 48),
    -3: (1328, 0, 80),
}
AWAYS = tuple(SENDS)
GRID_COPIES = 4
LOG2E = 1.4426950408889634
F32 = jnp.float32
BF16 = jnp.bfloat16
MESH = pl.DeviceIdType.MESH


def dot(a, b):
    return jnp.dot(a, b, preferred_element_type=F32)


def span_of(start, size, unit):
    return pl.ds(pl.multiple_of(start, unit), size)


def encode_kernel(
    regions,
    shards,
    used,
    source,
    target,
    bias,
    gain,
    grid_hbm,
    nodes_hbm,
    row_hbm,
    node_hbm,
    edge_hbm,
    attn_hbm,
    queries,
    keys,
    values,
    state,
    bounds,
    grid,
    row_weight,
    node_weight,
    edge_weight,
    attn_weight,
    projected,
    table,
    onehot,
    picks,
    hidden,
    sums,
    nodes,
    load_sem,
    row_send,
    row_recv,
    node_send,
    node_recv,
    sum_send,
    sum_recv,
):
    rows, width = grid.shape
    tile = state.shape[0]
    blocks, edges = source.shape
    part = rows // regions
    tiles = regions * shards
    region, shard = lax.axis_index("region"), lax.axis_index("shard")
    me = region * shards + shard

    def there(away):
        return (me + away >= 0) & (me + away < tiles)

    def device(away):
        return ((me + away) // shards, lax.rem(me + away, shards))

    def peer(step):
        return lax.rem(region + step, regions)

    loads = []
    piece = rows // GRID_COPIES

    def load(source_ref, target_ref):
        copy = pltpu.make_async_copy(source_ref, target_ref, load_sem.at[len(loads)])
        copy.start()
        loads.append(copy)
        return copy

    row_load = load(row_hbm, row_weight)
    grid_loads = [
        load(grid_hbm.at[pl.ds(i * piece, piece), :], grid.at[pl.ds(i * piece, piece), :])
        for i in range(GRID_COPIES)
    ]
    node_load = load(nodes_hbm, nodes.at[pl.ds(OWN, tile), :])
    node_weight_load = load(node_hbm, node_weight)
    edge_load = load(edge_hbm, edge_weight)
    attn_load = load(attn_hbm, attn_weight)

    barrier = pltpu.get_barrier_semaphore()
    for step in range(1, regions):
        pl.semaphore_signal(barrier, inc=1, device_id=(peer(step), shard), device_id_type=MESH)
    for away in AWAYS:
        near = lax.rem(me + away + tiles, tiles)
        pl.semaphore_signal(
            barrier, inc=1, device_id=(near // shards, lax.rem(near, shards)), device_id_type=MESH
        )

    row_load.wait()
    for i in range(GRID_COPIES):
        grid_loads[i].wait()
        projected[pl.ds(i * piece, piece), :] = dot(
            grid[pl.ds(i * piece, piece), :], row_weight[...]
        ).astype(BF16)
    node_load.wait()

    pl.semaphore_wait(barrier, regions - 1 + len(AWAYS))

    here = span_of(region * part, part, part)
    row_copies = []
    for step in sorted(range(1, regions), key=lambda k: -min(k, regions - k)):
        copy = pltpu.make_async_remote_copy(
            projected.at[span_of(peer(step) * part, part, part), :],
            table.at[here, :],
            row_send.at[step - 1],
            row_recv.at[step - 1],
            device_id=(peer(step), shard),
            device_id_type=MESH,
        )
        copy.start()
        row_copies.append(copy)

    def halo(held, sends, receives, away):
        there_row, own_row, count = SENDS[away]
        slot = AWAYS.index(away)
        return pltpu.make_async_remote_copy(
            held.at[pl.ds(OWN + own_row, count), :],
            held.at[pl.ds(there_row, count), :],
            sends.at[slot],
            receives.at[slot],
            device_id=device(away),
            device_id_type=MESH,
        )

    for away in AWAYS:

        @pl.when(there(away))
        def _():
            halo(nodes, node_send, node_recv, away).start()

    table[here, :] = projected[here, :]
    node_weight_load.wait()
    table[pl.ds(rows, tile), :] = (
        dot(nodes[pl.ds(OWN, tile), :], node_weight[...]) + bias[...]
    ).astype(BF16)
    source_cols = jnp.transpose(source[...])
    target_cols = jnp.transpose(target[...])
    lane_rows = lax.broadcasted_iota(jnp.int32, (edges, rows), 1)
    lane_tile = lax.broadcasted_iota(jnp.int32, (edges, tile), 1)
    sub_tile = lax.broadcasted_iota(jnp.int32, (tile, edges), 0)
    for block in range(blocks):
        span = pl.ds(block * edges, edges)
        onehot[span, pl.ds(0, rows)] = (
            (source_cols[:, block : block + 1] == lane_rows).astype(F32).astype(BF16)
        )
        onehot[span, pl.ds(rows, tile)] = (
            (target_cols[:, block : block + 1] == lane_tile).astype(F32).astype(BF16)
        )
        goal = jnp.where(used[...] > block, target[block : block + 1, :], -1)
        picks[:, span] = (goal == sub_tile).astype(F32).astype(BF16)

    for copy in row_copies:
        copy.wait()
    step_edges = 2 * edges
    for index in range(blocks * edges // step_edges):
        span = pl.ds(index * step_edges, step_edges)
        pre = dot(onehot[span, :], table[...])
        hidden[span, :] = (0.5 * pre * (1.0 + jnp.tanh(0.5 * pre))).astype(BF16)
    sums[pl.ds(OWN, tile), :] = dot(picks[...], hidden[...]).astype(BF16)
    for away in AWAYS:

        @pl.when(there(away))
        def _():
            halo(sums, sum_send, sum_recv, away).start()

    edge_load.wait()
    attn_load.wait()

    def normalised(span):
        held = (nodes[span, :].astype(F32) + dot(sums[span, :], edge_weight[...])).astype(BF16)
        wide = held.astype(F32)
        centred = wide - jnp.mean(wide, axis=1, keepdims=True)
        spread = jnp.mean(centred * centred, axis=1, keepdims=True)
        return held, (centred * lax.rsqrt(spread + 1e-05) * gain[...]).astype(BF16)

    def project(normed, span, flag):
        key = dot(normed, attn_weight[:, width : 2 * width])
        value = dot(normed, attn_weight[:, 2 * width :]) * flag
        for pair in range(width // 128):
            lanes = slice(pair * 128, pair * 128 + 128)
            keys[pair, span, :] = key[:, lanes].astype(BF16)
            values[pair, span, :] = value[:, lanes].astype(BF16)
        return (
            jnp.max(key * key, axis=0, keepdims=True),
            jnp.max(jnp.abs(value), axis=0, keepdims=True),
        )

    held, normed = normalised(pl.ds(OWN, tile))
    state[...] = held
    query = dot(normed, attn_weight[:, :width]) * (LOG2E * 0.125)
    for pair in range(width // 128):
        queries[pair, :, :] = query[:, pair * 128 : pair * 128 + 128].astype(BF16)
    top_key, top_value = project(normed, pl.ds(OWN, tile), 1.0)
    heads = (
        lax.broadcasted_iota(jnp.int32, (width, 128), 0) // 64
        == lax.broadcasted_iota(jnp.int32, (width, 128), 1)
    )
    heads = heads.astype(F32).astype(BF16)
    query_norm = jnp.max(dot((query * query).astype(BF16), heads), axis=0, keepdims=True)

    for first, count, away in CHUNKS:
        span = pl.ds(first, count)

        @pl.when(there(away))
        def _():
            halo(nodes, node_send, node_recv, -away).wait_recv()
            halo(sums, sum_send, sum_recv, -away).wait_recv()

        @pl.when(jnp.logical_not(there(away)))
        def _():
            nodes[span, :] = nodes[pl.ds(OWN, count), :]
            sums[span, :] = sums[pl.ds(OWN, count), :]

        _, normed = normalised(span)
        new_key, new_value = project(normed, span, there(away).astype(F32))
        top_key, top_value = jnp.maximum(top_key, new_key), jnp.maximum(top_value, new_value)

    key_norm = dot(jnp.broadcast_to(top_key, (8, width)).astype(BF16), heads)
    bounds[0:8, :] = query_norm * key_norm
    bounds[8:16, :] = jnp.broadcast_to(jnp.max(top_value, axis=1, keepdims=True), (8, 128))
    for away in AWAYS:

        @pl.when(there(away))
        def _():
            halo(nodes, node_send, node_recv, away).wait_send()
            halo(sums, sum_send, sum_recv, away).wait_send()


def window_kernel(
    bounds, queries_hbm, keys_hbm, values_hbm, state, out_hbm, mixed,
    queries, keys, values, out_weight, attended, ones, sems,
):
    pairs, tile, lanes = queries.shape
    half = tile // 2
    span_keys = KEYS - half
    tiles = lax.axis_size("region") * lax.axis_size("shard")
    me = lax.axis_index("region") * lax.axis_size("shard") + lax.axis_index("shard")

    def fetch(pair):
        return [
            pltpu.make_async_copy(held.at[pair], kept.at[pair], sems.at[slot, pair])
            for slot, (held, kept) in enumerate(
                ((queries_hbm, queries), (keys_hbm, keys), (values_hbm, values))
            )
        ]

    for pair in range(pairs):
        for copy in fetch(pair):
            copy.start()
    weight_copy = pltpu.make_async_copy(out_hbm, out_weight, sems.at[3, 0])
    weight_copy.start()

    spot = lax.broadcasted_iota(jnp.int32, (KEYS, lanes), 0) - OWN + me * tile
    ones[...] = ((spot >= 0) & (spot < tiles * tile)).astype(F32).astype(BF16)
    lane = lax.broadcasted_iota(jnp.int32, (half, lanes), 1)
    row = lax.broadcasted_iota(jnp.int32, (2 * half, lanes), 0) % half
    key = lax.broadcasted_iota(jnp.int32, (2 * half, lanes), 1)
    low = key >= row
    edge = (2 * HALF) // lanes * lanes
    high = [key + at < row + 2 * HALF for at in range(edge, span_keys, lanes)]
    small = jnp.max(bounds[0:8, :]) < 6400.0
    small = small & (jnp.max(bounds[8:16, :]) < 1e9)

    def attend(pair, part, with_max):
        rows = slice(part * half, part * half + half)
        query = queries[pair, rows, :]
        zero = jnp.zeros_like(query)
        query = jnp.concatenate(
            [jnp.where(lane < 64, query, zero), jnp.where(lane >= 64, query, zero)], axis=0
        )
        near = pl.ds(part * half, span_keys)
        scores = lax.dot_general(
            query, keys[pair, near, :], (((1,), (1,)), ((), ())), preferred_element_type=F32
        )
        scores = jnp.concatenate(
            [jnp.where(low, scores[:, :lanes], -1e30), scores[:, lanes:edge]]
            + [
                jnp.where(keep, scores[:, edge + i * lanes : edge + (i + 1) * lanes], -1e30)
                for i, keep in enumerate(high)
            ],
            axis=1,
        )
        if with_max:
            scores = scores - jnp.max(scores, axis=1, keepdims=True)
            raised = jnp.exp2(scores)
            live = lax.dot_general(
                raised.astype(BF16), ones[near, :], (((1,), (0,)), ((), ())),
                preferred_element_type=F32,
            )
            weights = (raised / live[:, 0:1]).astype(BF16)
            both = dot(weights, values[pair, near, :])
        else:
            raised = jnp.exp2(scores).astype(BF16)
            both = dot(raised, jnp.concatenate([values[pair, near, :], ones[near, :]], axis=1))
            both = both[:, :lanes] / both[:, lanes:]
        attended[rows, span_of(pair * lanes, lanes, lanes)] = jnp.where(
            lane < 64, both[:half], both[half:]
        ).astype(BF16)

    def both_halves(with_max, pair, carry):
        for copy in fetch(pair):
            copy.wait()
        for part in range(2):
            attend(pair, part, with_max)
        return carry

    @pl.when(small)
    def _():
        lax.fori_loop(0, pairs, functools.partial(both_halves, False), 0, unroll=2)

    @pl.when(jnp.logical_not(small))
    def _():
        lax.fori_loop(0, pairs, functools.partial(both_halves, True), 0)

    weight_copy.wait()
    mixed[...] = (state[...].astype(F32) + dot(attended[...], out_weight[...])).astype(BF16)


VMEM = pl.BlockSpec(memory_space=pltpu.VMEM)
ANY = pl.BlockSpec(memory_space=pl.ANY)


def local(
    grid_rows,
    node_inputs,
    row_weight,
    node_weight,
    edge_bias,
    edge_out_weight,
    norm_gain,
    attn_weight,
    attn_out_weight,
    edge_source,
    edge_target,
    block_count,
):
    tile, width = node_inputs.shape
    rows = grid_rows.shape[0]
    hidden = row_weight.shape[1]
    blocks, edges = edge_source.shape
    regions, shards = lax.axis_size("region"), lax.axis_size("shard")
    pairs = width // 128
    dma = pltpu.SemaphoreType.DMA
    queries, keys, values, state, bounds = pl.pallas_call(
        functools.partial(encode_kernel, regions, shards),
        out_shape=(
            jax.ShapeDtypeStruct((pairs, tile, 128), BF16),
            jax.ShapeDtypeStruct((pairs, KEYS, 128), BF16),
            jax.ShapeDtypeStruct((pairs, KEYS, 128), BF16),
            jax.ShapeDtypeStruct((tile, width), BF16),
            jax.ShapeDtypeStruct((16, 128), F32),
        ),
        in_specs=[VMEM] * 5 + [ANY] * 6,
        out_specs=[VMEM] * 5,
        scratch_shapes=[
            pltpu.VMEM((rows, width), BF16),
            pltpu.VMEM(row_weight.shape, BF16),
            pltpu.VMEM(node_weight.shape, BF16),
            pltpu.VMEM(edge_out_weight.shape, BF16),
            pltpu.VMEM(attn_weight.shape, BF16),
            pltpu.VMEM((rows, hidden), BF16),
            pltpu.VMEM((rows + tile, hidden), BF16),
            pltpu.VMEM((blocks * edges, rows + tile), BF16),
            pltpu.VMEM((tile, blocks * edges), BF16),
            pltpu.VMEM((blocks * edges, hidden), BF16),
            pltpu.VMEM((KEYS, hidden), BF16),
            pltpu.VMEM((KEYS, width), BF16),
            dma((GRID_COPIES + 5,)),
            dma((regions - 1,)),
            dma((regions - 1,)),
            dma((len(AWAYS),)),
            dma((len(AWAYS),)),
            dma((len(AWAYS),)),
            dma((len(AWAYS),)),
        ],
        compiler_params=pltpu.CompilerParams(collective_id=0, has_side_effects=True),
        name="encode",
    )(
        jnp.broadcast_to(block_count[:, None], (1, edges)),
        edge_source,
        edge_target,
        edge_bias[None],
        norm_gain[None],
        grid_rows,
        node_inputs,
        row_weight,
        node_weight,
        edge_out_weight,
        attn_weight,
    )
    return pl.pallas_call(
        window_kernel,
        out_shape=jax.ShapeDtypeStruct((tile, width), BF16),
        in_specs=[VMEM, ANY, ANY, ANY, VMEM, ANY],
        out_specs=VMEM,
        scratch_shapes=[
            pltpu.VMEM((pairs, tile, 128), BF16),
            pltpu.VMEM((pairs, KEYS, 128), BF16),
            pltpu.VMEM((pairs, KEYS, 128), BF16),
            pltpu.VMEM((width, width), BF16),
            pltpu.VMEM((tile, width), BF16),
            pltpu.VMEM((KEYS, 128), BF16),
            dma((4, pairs)),
        ],
        name="window",
    )(bounds, queries, keys, values, state, attn_out_weight)


def solution(mesh):
    placed = (
        P(("region", "shard"), None),
        P(("region", "shard"), None),
        P(),
        P(),
        P(),
        P(),
        P(),
        P(),
        P(),
        P(("region", "shard"), None),
        P(("region", "shard"), None),
        P(("region", "shard")),
    )
    return jax.shard_map(
        local, mesh=mesh, in_specs=placed, out_specs=P(("region", "shard"), None), check_vma=False
    )
```

```python
import functools

import jax
import jax.numpy as jnp
from jax import lax
from jax.experimental import pallas as pl
from jax.experimental.pallas import tpu as pltpu
from jax.sharding import PartitionSpec as P

HALF = 560
KEYS = 1408
OWN = 560
PLACES = {-1: (304, 256), 1: (816, 256), -2: (48, 256), 2: (1072, 256), -3: (0, 48), 3: (1328, 80)}
SLOTS = tuple(PLACES)
GRID_COPIES = 4
ACROSS = 4
LOG2E = 1.4426950408889634
F32 = jnp.float32
BF16 = jnp.bfloat16
MESH = pl.DeviceIdType.MESH


def dot(a, b):
    return jnp.dot(a, b, preferred_element_type=F32)


def span_of(start, size, unit):
    return pl.ds(pl.multiple_of(start, unit), size)


def encode_kernel(
    regions,
    shards,
    used,
    source,
    target,
    bias,
    gain,
    grid_hbm,
    nodes_hbm,
    row_hbm,
    node_hbm,
    edge_hbm,
    attn_hbm,
    queries,
    keys,
    values,
    state,
    bounds,
    grid,
    row_weight,
    node_weight,
    edge_weight,
    attn_weight,
    projected,
    table,
    onehot,
    picks,
    hidden,
    sums,
    nodes,
    load_sem,
    row_send,
    row_recv,
    node_send,
    node_recv,
    sum_send,
    sum_recv,
):
    rows, width = grid.shape
    tile = state.shape[0]
    blocks, edges = source.shape
    part = rows // regions
    tiles = regions * shards
    region, shard = lax.axis_index("region"), lax.axis_index("shard")
    me = region * shards + shard

    def there(away):
        return (me + away >= 0) & (me + away < tiles)

    def device(away):
        return ((me + away) // shards, lax.rem(me + away, shards))

    def peer(step):
        return lax.rem(region + step, regions)

    loads = []
    piece = rows // GRID_COPIES

    def load(source_ref, target_ref):
        copy = pltpu.make_async_copy(source_ref, target_ref, load_sem.at[len(loads)])
        copy.start()
        loads.append(copy)
        return copy

    row_load = load(row_hbm, row_weight)
    grid_loads = [
        load(grid_hbm.at[pl.ds(i * piece, piece), :], grid.at[pl.ds(i * piece, piece), :])
        for i in range(GRID_COPIES)
    ]
    node_load = load(nodes_hbm, nodes.at[pl.ds(OWN, tile), :])
    node_weight_load = load(node_hbm, node_weight)
    edge_load = load(edge_hbm, edge_weight)
    attn_load = load(attn_hbm, attn_weight)

    barrier = pltpu.get_barrier_semaphore()
    for step in range(1, regions):
        pl.semaphore_signal(barrier, inc=1, device_id=(peer(step), shard), device_id_type=MESH)
    for away in SLOTS:
        near = lax.rem(me + away + tiles, tiles)
        pl.semaphore_signal(
            barrier, inc=1, device_id=(near // shards, lax.rem(near, shards)), device_id_type=MESH
        )

    row_load.wait()
    for i in range(GRID_COPIES):
        grid_loads[i].wait()
        projected[pl.ds(i * piece, piece), :] = dot(
            grid[pl.ds(i * piece, piece), :], row_weight[...]
        ).astype(BF16)
    node_load.wait()

    pl.semaphore_wait(barrier, regions - 1 + len(SLOTS))

    here = span_of(region * part, part, part)
    row_copies = []
    for step in sorted(range(1, regions), key=lambda k: -min(k, regions - k)):
        copy = pltpu.make_async_remote_copy(
            projected.at[span_of(peer(step) * part, part, part), :],
            table.at[here, :],
            row_send.at[step - 1],
            row_recv.at[step - 1],
            device_id=(peer(step), shard),
            device_id_type=MESH,
        )
        copy.start()
        row_copies.append(copy)

    first_core = lax.rem(shard, 2) == 0
    partner = 1 - 2 * lax.rem(shard, 2)

    def halo(kind, slot, away, first):
        held, sends, receives = kind
        row, count = PLACES[slot]
        at = SLOTS.index(slot)
        return pltpu.make_async_remote_copy(
            held.at[pl.ds(first, count), :],
            held.at[pl.ds(row, count), :],
            sends.at[at],
            receives.at[at],
            device_id=device(away),
            device_id_type=MESH,
        )

    node_halo = (nodes, node_send, node_recv)
    sum_halo = (sums, sum_send, sum_recv)

    def first_copies(kind):
        return [
            (there(2), halo(kind, -2, 2, OWN)),
            (there(-2), halo(kind, 2, -2, OWN)),
            (first_core, halo(kind, -1, 1, OWN)),
            (jnp.logical_not(first_core), halo(kind, 1, -1, OWN)),
        ]

    def forwards(kind, came):
        if came < 0:
            return [
                (there(-2) & jnp.logical_not(first_core), halo(kind, -1, -1, PLACES[-2][0])),
                (there(-2) & there(1), halo(kind, -3, 1, PLACES[-2][0] + tile - PLACES[-3][1])),
            ]
        return [
            (there(2) & first_core, halo(kind, 1, 1, PLACES[2][0])),
            (there(2) & there(-1), halo(kind, 3, -1, PLACES[2][0])),
        ]

    def start(copies):
        for condition, copy in copies:
            pl.when(condition)(copy.start)

    start(first_copies(node_halo))

    table[here, :] = projected[here, :]
    node_weight_load.wait()
    table[pl.ds(rows, tile), :] = (
        dot(nodes[pl.ds(OWN, tile), :], node_weight[...]) + bias[...]
    ).astype(BF16)
    source_cols = jnp.transpose(source[...])
    target_cols = jnp.transpose(target[...])
    lane_rows = lax.broadcasted_iota(jnp.int32, (edges, rows), 1)
    lane_tile = lax.broadcasted_iota(jnp.int32, (edges, tile), 1)
    sub_tile = lax.broadcasted_iota(jnp.int32, (tile, edges), 0)
    limit = jnp.full((1, edges), used[0], jnp.int32)
    for block in range(blocks):
        span = pl.ds(block * edges, edges)
        onehot[span, pl.ds(0, rows)] = (
            (source_cols[:, block : block + 1] == lane_rows).astype(F32).astype(BF16)
        )
        onehot[span, pl.ds(rows, tile)] = (
            (target_cols[:, block : block + 1] == lane_tile).astype(F32).astype(BF16)
        )
        goal = jnp.where(limit > block, target[block : block + 1, :], -1)
        picks[:, span] = (goal == sub_tile).astype(F32).astype(BF16)

    for copy in row_copies:
        copy.wait()
    step_edges = 2 * edges
    for index in range(blocks * edges // step_edges):
        span = pl.ds(index * step_edges, step_edges)
        pre = dot(onehot[span, :], table[...])
        hidden[span, :] = (0.5 * pre * (1.0 + jnp.tanh(0.5 * pre))).astype(BF16)
    sums[pl.ds(OWN, tile), :] = dot(picks[...], hidden[...]).astype(BF16)
    start(first_copies(sum_halo))

    edge_load.wait()
    attn_load.wait()

    def take(ref, spans):
        return jnp.concatenate([ref[span, :] for span in spans], axis=0)

    def normalised(spans):
        held = take(nodes, spans).astype(F32) + dot(take(sums, spans), edge_weight[...])
        held = held.astype(BF16)
        wide = held.astype(F32)
        centred = wide - jnp.mean(wide, axis=1, keepdims=True)
        spread = jnp.mean(centred * centred, axis=1, keepdims=True)
        return held, (centred * lax.rsqrt(spread + 1e-05) * gain[...]).astype(BF16)

    def project(normed, spans, flags):
        key = dot(normed, attn_weight[:, width : 2 * width])
        value = dot(normed, attn_weight[:, 2 * width :])
        begin = 0
        for span, flag in zip(spans, flags):
            rows_in = slice(begin, begin + span.size)
            begin += span.size
            for pair in range(width // 128):
                lanes = slice(pair * 128, pair * 128 + 128)
                keys[pair, span, :] = key[rows_in, lanes].astype(BF16)
                some = value[rows_in, lanes]
                values[pair, span, :] = (some if flag is None else some * flag).astype(BF16)
        return (
            jnp.max(key * key, axis=0, keepdims=True),
            jnp.max(jnp.abs(value), axis=0, keepdims=True),
        )

    own = pl.ds(OWN, tile)
    held, normed = normalised([own])
    state[...] = held
    query = dot(normed, attn_weight[:, :width]) * (LOG2E * 0.125)
    for pair in range(width // 128):
        queries[pair, :, :] = query[:, pair * 128 : pair * 128 + 128].astype(BF16)
    tops = project(normed, [own], [None])
    heads = (
        lax.broadcasted_iota(jnp.int32, (width, 128), 0) // 64
        == lax.broadcasted_iota(jnp.int32, (width, 128), 1)
    )
    heads = heads.astype(F32).astype(BF16)
    query_norm = jnp.max(dot((query * query).astype(BF16), heads), axis=0, keepdims=True)

    def arrive(slot):
        row, count = PLACES[slot]
        span = pl.ds(row, count)

        @pl.when(there(slot))
        def _():
            halo(node_halo, slot, 0, row).wait_recv()
            halo(sum_halo, slot, 0, row).wait_recv()

        @pl.when(jnp.logical_not(there(slot)))
        def _():
            nodes[span, :] = nodes[pl.ds(OWN, count), :]
            sums[span, :] = sums[pl.ds(OWN, count), :]

    def encode(spans, flags, tops):
        _, normed = normalised(spans)
        return tuple(jnp.maximum(a, b) for a, b in zip(tops, project(normed, spans, flags)))

    def choose(picks):
        row, flag = jnp.int32(0), F32(0)
        for condition, slot in picks:
            if abs(slot) == 1:
                pl.when(condition)(functools.partial(arrive, slot))
            row = jnp.where(condition, PLACES[slot][0], row)
            flag = jnp.where(condition, there(slot).astype(F32), flag)
        return [pl.ds(pl.multiple_of(row, 16), tile)], [flag]

    def far(slot):
        arrive(slot)
        for condition, copy in forwards(node_halo, slot) + forwards(sum_halo, slot):
            pl.when(condition)(copy.start)

    second_core = jnp.logical_not(first_core)
    tops = encode(*choose([(first_core, 1), (second_core, -1)]), tops)
    across, down = lax.rem(region, ACROSS), shard // 2
    late_low = (across == 0) & (down == 0)
    late_high = jnp.logical_not(late_low)
    crossing = late_low | ((across == ACROSS - 1) & (down == shards // 2 - 1))

    def far_late(condition):
        pl.when(condition & late_low)(functools.partial(far, -2))
        pl.when(condition & late_high)(functools.partial(far, 2))

    pl.when(late_low)(functools.partial(far, 2))
    pl.when(late_high)(functools.partial(far, -2))
    far_late(jnp.logical_not(crossing))
    row = jnp.where(late_low, PLACES[2][0], PLACES[-2][0])
    flag = jnp.where(late_low, there(2).astype(F32), there(-2).astype(F32))
    tops = encode([pl.ds(pl.multiple_of(row, 16), tile)], [flag], tops)
    early = late_low ^ first_core
    far_late(crossing & jnp.logical_not(early))
    tops = encode(
        *choose(
            [
                (early & first_core, -1),
                (early & second_core, 1),
                (jnp.logical_not(early) & late_low, -2),
                (jnp.logical_not(early) & late_high, 2),
            ]
        ),
        tops,
    )
    far_late(crossing & early)
    tops = encode(
        *choose(
            [
                (jnp.logical_not(early) & first_core, -1),
                (jnp.logical_not(early) & second_core, 1),
                (early & late_low, -2),
                (early & late_high, 2),
            ]
        ),
        tops,
    )
    last = [-3, 3]
    for slot in last:
        arrive(slot)
    tops = encode([pl.ds(*PLACES[slot]) for slot in last], [there(slot).astype(F32) for slot in last], tops)

    top_key, top_value = tops
    key_norm = dot(jnp.broadcast_to(top_key, (8, width)).astype(BF16), heads)
    bounds[0:8, :] = query_norm * key_norm
    bounds[8:16, :] = jnp.broadcast_to(jnp.max(top_value, axis=1, keepdims=True), (8, 128))
    for kind in (node_halo, sum_halo):
        for condition, copy in first_copies(kind) + forwards(kind, -2) + forwards(kind, 2):
            pl.when(condition)(copy.wait_send)


def window_kernel(
    bounds, queries, keys, values, state, out_hbm, mixed,
    out_weight, attended, ones, sem,
):
    pairs, tile, lanes = queries.shape
    half = tile // 2
    span_keys = KEYS - half
    tiles = lax.axis_size("region") * lax.axis_size("shard")
    me = lax.axis_index("region") * lax.axis_size("shard") + lax.axis_index("shard")

    weight_copy = pltpu.make_async_copy(out_hbm, out_weight, sem)
    weight_copy.start()

    spot = lax.broadcasted_iota(jnp.int32, (KEYS, lanes), 0) - OWN + me * tile
    ones[...] = ((spot >= 0) & (spot < tiles * tile)).astype(F32).astype(BF16)
    lane = lax.broadcasted_iota(jnp.int32, (half, lanes), 1)
    row = lax.broadcasted_iota(jnp.int32, (2 * half, lanes), 0) % half
    key = lax.broadcasted_iota(jnp.int32, (2 * half, lanes), 1)
    low = key >= row
    edge = (2 * HALF) // lanes * lanes
    high = [key + at < row + 2 * HALF for at in range(edge, span_keys, lanes)]
    small = jnp.max(bounds[0:8, :]) < 6400.0
    small = small & (jnp.max(bounds[8:16, :]) < 1e9)

    def attend(pair, part, with_max):
        rows = slice(part * half, part * half + half)
        query = queries[pair, rows, :]
        zero = jnp.zeros_like(query)
        query = jnp.concatenate(
            [jnp.where(lane < 64, query, zero), jnp.where(lane >= 64, query, zero)], axis=0
        )
        near = pl.ds(part * half, span_keys)
        scores = lax.dot_general(
            query, keys[pair, near, :], (((1,), (1,)), ((), ())), preferred_element_type=F32
        )
        scores = jnp.concatenate(
            [jnp.where(low, scores[:, :lanes], -1e30), scores[:, lanes:edge]]
            + [
                jnp.where(keep, scores[:, edge + i * lanes : edge + (i + 1) * lanes], -1e30)
                for i, keep in enumerate(high)
            ],
            axis=1,
        )
        if with_max:
            scores = scores - jnp.max(scores, axis=1, keepdims=True)
            raised = jnp.exp2(scores)
            live = lax.dot_general(
                raised.astype(BF16), ones[near, :], (((1,), (0,)), ((), ())),
                preferred_element_type=F32,
            )
            weights = (raised / live[:, 0:1]).astype(BF16)
            both = dot(weights, values[pair, near, :])
        else:
            raised = jnp.exp2(scores).astype(BF16)
            both = dot(raised, jnp.concatenate([values[pair, near, :], ones[near, :]], axis=1))
            both = both[:, :lanes] / both[:, lanes:]
        attended[rows, span_of(pair * lanes, lanes, lanes)] = jnp.where(
            lane < 64, both[:half], both[half:]
        ).astype(BF16)

    def both_halves(with_max, pair, carry):
        for part in range(2):
            attend(pair, part, with_max)
        return carry

    @pl.when(small)
    def _():
        lax.fori_loop(0, pairs, functools.partial(both_halves, False), 0, unroll=4)

    @pl.when(jnp.logical_not(small))
    def _():
        lax.fori_loop(0, pairs, functools.partial(both_halves, True), 0)

    weight_copy.wait()
    mixed[...] = (state[...].astype(F32) + dot(attended[...], out_weight[...])).astype(BF16)


VMEM = pl.BlockSpec(memory_space=pltpu.VMEM)
ANY = pl.BlockSpec(memory_space=pl.ANY)


def local(
    grid_rows,
    node_inputs,
    row_weight,
    node_weight,
    edge_bias,
    edge_out_weight,
    norm_gain,
    attn_weight,
    attn_out_weight,
    edge_source,
    edge_target,
    block_count,
):
    tile, width = node_inputs.shape
    rows = grid_rows.shape[0]
    hidden = row_weight.shape[1]
    blocks, edges = edge_source.shape
    regions, shards = lax.axis_size("region"), lax.axis_size("shard")
    pairs = width // 128
    dma = pltpu.SemaphoreType.DMA
    queries, keys, values, state, bounds = pl.pallas_call(
        functools.partial(encode_kernel, regions, shards),
        out_shape=(
            pltpu.VMEM((pairs, tile, 128), BF16),
            pltpu.VMEM((pairs, KEYS, 128), BF16),
            pltpu.VMEM((pairs, KEYS, 128), BF16),
            pltpu.VMEM((tile, width), BF16),
            jax.ShapeDtypeStruct((16, 128), F32),
        ),
        in_specs=[pl.BlockSpec(memory_space=pltpu.SMEM)] + [VMEM] * 4 + [ANY] * 6,
        out_specs=[VMEM] * 5,
        scratch_shapes=[
            pltpu.VMEM((rows, width), BF16),
            pltpu.VMEM(row_weight.shape, BF16),
            pltpu.VMEM(node_weight.shape, BF16),
            pltpu.VMEM(edge_out_weight.shape, BF16),
            pltpu.VMEM(attn_weight.shape, BF16),
            pltpu.VMEM((rows, hidden), BF16),
            pltpu.VMEM((rows + tile, hidden), BF16),
            pltpu.VMEM((blocks * edges, rows + tile), BF16),
            pltpu.VMEM((tile, blocks * edges), BF16),
            pltpu.VMEM((blocks * edges, hidden), BF16),
            pltpu.VMEM((KEYS, hidden), BF16),
            pltpu.VMEM((KEYS, width), BF16),
            dma((GRID_COPIES + 5,)),
            dma((regions - 1,)),
            dma((regions - 1,)),
            dma((len(SLOTS),)),
            dma((len(SLOTS),)),
            dma((len(SLOTS),)),
            dma((len(SLOTS),)),
        ],
        compiler_params=pltpu.CompilerParams(
            collective_id=0, has_side_effects=True, vmem_limit_bytes=57 * 2**20
        ),
        name="encode",
    )(
        block_count,
        edge_source,
        edge_target,
        edge_bias[None],
        norm_gain[None],
        grid_rows,
        node_inputs,
        row_weight,
        node_weight,
        edge_out_weight,
        attn_weight,
    )
    return pl.pallas_call(
        window_kernel,
        out_shape=jax.ShapeDtypeStruct((tile, width), BF16),
        in_specs=[VMEM] * 5 + [ANY],
        out_specs=VMEM,
        scratch_shapes=[
            pltpu.VMEM((width, width), BF16),
            pltpu.VMEM((tile, width), BF16),
            pltpu.VMEM((KEYS, 128), BF16),
            dma,
        ],
        compiler_params=pltpu.CompilerParams(vmem_limit_bytes=57 * 2**20),
        name="window",
    )(bounds, queries, keys, values, state, attn_out_weight)


def solution(mesh):
    placed = (
        P(("region", "shard"), None),
        P(("region", "shard"), None),
        P(),
        P(),
        P(),
        P(),
        P(),
        P(),
        P(),
        P(("region", "shard"), None),
        P(("region", "shard"), None),
        P(("region", "shard")),
    )
    return jax.shard_map(
        local, mesh=mesh, in_specs=placed, out_specs=P(("region", "shard"), None), check_vma=False
    )
```

```python
import functools

import jax
import jax.numpy as jnp
from jax import lax
from jax.experimental import pallas as pl
from jax.experimental.pallas import tpu as pltpu
from jax.sharding import PartitionSpec as P

HALF = 560
KEYS = 1408
OWN = 560
PLACES = {-1: (304, 256), 1: (816, 256), -2: (48, 256), 2: (1072, 256), -3: (0, 48), 3: (1328, 80)}
SLOTS = tuple(PLACES)
GRID_COPIES = 4
ACROSS = 4
LOG2E = 1.4426950408889634
F32 = jnp.float32
BF16 = jnp.bfloat16
MESH = pl.DeviceIdType.MESH


def dot(a, b):
    return jnp.dot(a, b, preferred_element_type=F32)


def span_of(start, size, unit):
    return pl.ds(pl.multiple_of(start, unit), size)


def encode_kernel(
    regions,
    shards,
    used,
    source,
    target,
    bias,
    gain,
    grid_hbm,
    nodes_hbm,
    row_hbm,
    node_hbm,
    edge_hbm,
    attn_hbm,
    out_hbm,
    queries,
    keys,
    values,
    state,
    bounds,
    out_weight,
    grid,
    row_weight,
    node_weight,
    edge_weight,
    attn_weight,
    projected,
    table,
    onehot,
    picks,
    hidden,
    sums,
    nodes,
    load_sem,
    row_send,
    row_recv,
    node_send,
    node_recv,
    sum_send,
    sum_recv,
):
    rows, width = grid.shape
    tile = state.shape[0]
    blocks, edges = source.shape
    part = rows // regions
    tiles = regions * shards
    region, shard = lax.axis_index("region"), lax.axis_index("shard")
    me = region * shards + shard

    def there(away):
        return (me + away >= 0) & (me + away < tiles)

    def device(away):
        return ((me + away) // shards, lax.rem(me + away, shards))

    def peer(step):
        return lax.rem(region + step, regions)

    loads = []
    piece = rows // GRID_COPIES

    def load(source_ref, target_ref):
        copy = pltpu.make_async_copy(source_ref, target_ref, load_sem.at[len(loads)])
        copy.start()
        loads.append(copy)
        return copy

    row_load = load(row_hbm, row_weight)
    grid_loads = [
        load(grid_hbm.at[pl.ds(i * piece, piece), :], grid.at[pl.ds(i * piece, piece), :])
        for i in range(GRID_COPIES)
    ]
    node_load = load(nodes_hbm, nodes.at[pl.ds(OWN, tile), :])
    node_weight_load = load(node_hbm, node_weight)
    edge_load = load(edge_hbm, edge_weight)
    attn_load = load(attn_hbm, attn_weight)
    out_load = load(out_hbm, out_weight)

    barrier = pltpu.get_barrier_semaphore()
    for step in range(1, regions):
        pl.semaphore_signal(barrier, inc=1, device_id=(peer(step), shard), device_id_type=MESH)
    for away in SLOTS:
        near = lax.rem(me + away + tiles, tiles)
        pl.semaphore_signal(
            barrier, inc=1, device_id=(near // shards, lax.rem(near, shards)), device_id_type=MESH
        )

    row_load.wait()
    for i in range(GRID_COPIES):
        grid_loads[i].wait()
        projected[pl.ds(i * piece, piece), :] = dot(
            grid[pl.ds(i * piece, piece), :], row_weight[...]
        ).astype(BF16)
    node_load.wait()

    pl.semaphore_wait(barrier, regions - 1 + len(SLOTS))

    here = span_of(region * part, part, part)
    row_copies = []
    for step in sorted(range(1, regions), key=lambda k: -min(k, regions - k)):
        copy = pltpu.make_async_remote_copy(
            projected.at[span_of(peer(step) * part, part, part), :],
            table.at[here, :],
            row_send.at[step - 1],
            row_recv.at[step - 1],
            device_id=(peer(step), shard),
            device_id_type=MESH,
        )
        copy.start()
        row_copies.append(copy)

    first_core = lax.rem(shard, 2) == 0
    partner = 1 - 2 * lax.rem(shard, 2)

    def halo(kind, slot, away, first):
        held, sends, receives = kind
        row, count = PLACES[slot]
        at = SLOTS.index(slot)
        return pltpu.make_async_remote_copy(
            held.at[pl.ds(first, count), :],
            held.at[pl.ds(row, count), :],
            sends.at[at],
            receives.at[at],
            device_id=device(away),
            device_id_type=MESH,
        )

    node_halo = (nodes, node_send, node_recv)
    sum_halo = (sums, sum_send, sum_recv)

    def first_copies(kind):
        return [
            (there(2), halo(kind, -2, 2, OWN)),
            (there(-2), halo(kind, 2, -2, OWN)),
            (first_core, halo(kind, -1, 1, OWN)),
            (jnp.logical_not(first_core), halo(kind, 1, -1, OWN)),
        ]

    def forwards(kind, came):
        if came < 0:
            return [
                (there(-2) & jnp.logical_not(first_core), halo(kind, -1, -1, PLACES[-2][0])),
                (there(-2) & there(1), halo(kind, -3, 1, PLACES[-2][0] + tile - PLACES[-3][1])),
            ]
        return [
            (there(2) & first_core, halo(kind, 1, 1, PLACES[2][0])),
            (there(2) & there(-1), halo(kind, 3, -1, PLACES[2][0])),
        ]

    def start(copies):
        for condition, copy in copies:
            pl.when(condition)(copy.start)

    start(first_copies(node_halo))

    table[here, :] = projected[here, :]
    node_weight_load.wait()
    table[pl.ds(rows, tile), :] = (
        dot(nodes[pl.ds(OWN, tile), :], node_weight[...]) + bias[...]
    ).astype(BF16)
    source_cols = jnp.transpose(source[...])
    target_cols = jnp.transpose(target[...])
    lane_rows = lax.broadcasted_iota(jnp.int32, (edges, rows), 1)
    lane_tile = lax.broadcasted_iota(jnp.int32, (edges, tile), 1)
    sub_tile = lax.broadcasted_iota(jnp.int32, (tile, edges), 0)
    limit = jnp.full((1, edges), used[0], jnp.int32)
    for block in range(blocks):
        span = pl.ds(block * edges, edges)
        onehot[span, pl.ds(0, rows)] = (
            (source_cols[:, block : block + 1] == lane_rows).astype(F32).astype(BF16)
        )
        onehot[span, pl.ds(rows, tile)] = (
            (target_cols[:, block : block + 1] == lane_tile).astype(F32).astype(BF16)
        )
        goal = jnp.where(limit > block, target[block : block + 1, :], -1)
        picks[:, span] = (goal == sub_tile).astype(F32).astype(BF16)

    for copy in row_copies:
        copy.wait()
    step_edges = 2 * edges
    for index in range(blocks * edges // step_edges):
        span = pl.ds(index * step_edges, step_edges)
        pre = dot(onehot[span, :], table[...])
        hidden[span, :] = (0.5 * pre * (1.0 + jnp.tanh(0.5 * pre))).astype(BF16)
    sums[pl.ds(OWN, tile), :] = dot(picks[...], hidden[...]).astype(BF16)
    start(first_copies(sum_halo))

    edge_load.wait()
    attn_load.wait()
    out_load.wait()

    def take(ref, spans):
        return jnp.concatenate([ref[span, :] for span in spans], axis=0)

    def normalised(spans):
        held = take(nodes, spans).astype(F32) + dot(take(sums, spans), edge_weight[...])
        held = held.astype(BF16)
        wide = held.astype(F32)
        centred = wide - jnp.mean(wide, axis=1, keepdims=True)
        spread = jnp.mean(centred * centred, axis=1, keepdims=True)
        return held, (centred * lax.rsqrt(spread + 1e-05) * gain[...]).astype(BF16)

    def project(normed, spans, flags):
        key = dot(normed, attn_weight[:, width : 2 * width])
        value = dot(normed, attn_weight[:, 2 * width :])
        begin = 0
        for span, flag in zip(spans, flags):
            rows_in = slice(begin, begin + span.size)
            begin += span.size
            for pair in range(width // 128):
                lanes = slice(pair * 128, pair * 128 + 128)
                keys[pair, span, :] = key[rows_in, lanes].astype(BF16)
                some = value[rows_in, lanes]
                values[pair, span, :] = (some if flag is None else some * flag).astype(BF16)
        return (
            jnp.max(key * key, axis=0, keepdims=True),
            jnp.max(jnp.abs(value), axis=0, keepdims=True),
        )

    own = pl.ds(OWN, tile)
    held, normed = normalised([own])
    state[...] = held
    query = dot(normed, attn_weight[:, :width]) * (LOG2E * 0.125)
    for pair in range(width // 128):
        queries[pair, :, :] = query[:, pair * 128 : pair * 128 + 128].astype(BF16)
    tops = project(normed, [own], [None])
    heads = (
        lax.broadcasted_iota(jnp.int32, (width, 128), 0) // 64
        == lax.broadcasted_iota(jnp.int32, (width, 128), 1)
    )
    heads = heads.astype(F32).astype(BF16)
    query_norm = jnp.max(dot((query * query).astype(BF16), heads), axis=0, keepdims=True)

    def arrive(slot):
        row, count = PLACES[slot]
        span = pl.ds(row, count)

        @pl.when(there(slot))
        def _():
            halo(node_halo, slot, 0, row).wait_recv()
            halo(sum_halo, slot, 0, row).wait_recv()

        @pl.when(jnp.logical_not(there(slot)))
        def _():
            nodes[span, :] = nodes[pl.ds(OWN, count), :]
            sums[span, :] = sums[pl.ds(OWN, count), :]

    def encode(spans, flags, tops):
        _, normed = normalised(spans)
        return tuple(jnp.maximum(a, b) for a, b in zip(tops, project(normed, spans, flags)))

    def choose(picks):
        row, flag = jnp.int32(0), F32(0)
        for condition, slot in picks:
            if abs(slot) == 1:
                pl.when(condition)(functools.partial(arrive, slot))
            row = jnp.where(condition, PLACES[slot][0], row)
            flag = jnp.where(condition, there(slot).astype(F32), flag)
        return [pl.ds(pl.multiple_of(row, 16), tile)], [flag]

    def far(slot):
        arrive(slot)
        for condition, copy in forwards(node_halo, slot) + forwards(sum_halo, slot):
            pl.when(condition)(copy.start)

    second_core = jnp.logical_not(first_core)
    tops = encode(*choose([(first_core, 1), (second_core, -1)]), tops)
    across, down = lax.rem(region, ACROSS), shard // 2
    late_low = (across == 0) & (down == 0)
    late_high = jnp.logical_not(late_low)
    crossing = late_low | ((across == ACROSS - 1) & (down == shards // 2 - 1))

    def far_late(condition):
        pl.when(condition & late_low)(functools.partial(far, -2))
        pl.when(condition & late_high)(functools.partial(far, 2))

    pl.when(late_low)(functools.partial(far, 2))
    pl.when(late_high)(functools.partial(far, -2))
    far_late(jnp.logical_not(crossing))
    row = jnp.where(late_low, PLACES[2][0], PLACES[-2][0])
    flag = jnp.where(late_low, there(2).astype(F32), there(-2).astype(F32))
    tops = encode([pl.ds(pl.multiple_of(row, 16), tile)], [flag], tops)
    early = late_low ^ first_core
    far_late(crossing & jnp.logical_not(early))
    tops = encode(
        *choose(
            [
                (early & first_core, -1),
                (early & second_core, 1),
                (jnp.logical_not(early) & late_low, -2),
                (jnp.logical_not(early) & late_high, 2),
            ]
        ),
        tops,
    )
    far_late(crossing & early)
    tops = encode(
        *choose(
            [
                (jnp.logical_not(early) & first_core, -1),
                (jnp.logical_not(early) & second_core, 1),
                (early & late_low, -2),
                (early & late_high, 2),
            ]
        ),
        tops,
    )
    last = [-3, 3]
    for slot in last:
        arrive(slot)
    tops = encode([pl.ds(*PLACES[slot]) for slot in last], [there(slot).astype(F32) for slot in last], tops)

    top_key, top_value = tops
    key_norm = dot(jnp.broadcast_to(top_key, (8, width)).astype(BF16), heads)
    bounds[0:8, :] = query_norm * key_norm
    bounds[8:16, :] = jnp.broadcast_to(jnp.max(top_value, axis=1, keepdims=True), (8, 128))
    for kind in (node_halo, sum_halo):
        for condition, copy in first_copies(kind) + forwards(kind, -2) + forwards(kind, 2):
            pl.when(condition)(copy.wait_send)


def window_kernel(
    bounds, queries, keys, values, state, out_weight, mixed,
    attended, ones,
):
    pairs, tile, lanes = queries.shape
    half = tile // 2
    span_keys = KEYS - half
    tiles = lax.axis_size("region") * lax.axis_size("shard")
    me = lax.axis_index("region") * lax.axis_size("shard") + lax.axis_index("shard")

    spot = lax.broadcasted_iota(jnp.int32, (KEYS, lanes), 0) - OWN + me * tile
    ones[...] = ((spot >= 0) & (spot < tiles * tile)).astype(F32).astype(BF16)
    lane = lax.broadcasted_iota(jnp.int32, (half, lanes), 1)
    row = lax.broadcasted_iota(jnp.int32, (2 * half, lanes), 0) % half
    key = lax.broadcasted_iota(jnp.int32, (2 * half, lanes), 1)
    low = key >= row
    edge = (2 * HALF) // lanes * lanes
    high = [key + at < row + 2 * HALF for at in range(edge, span_keys, lanes)]
    small = jnp.max(bounds[0:8, :]) < 6400.0
    small = small & (jnp.max(bounds[8:16, :]) < 1e9)

    def attend(pair, part, with_max):
        rows = slice(part * half, part * half + half)
        query = queries[pair, rows, :]
        zero = jnp.zeros_like(query)
        query = jnp.concatenate(
            [jnp.where(lane < 64, query, zero), jnp.where(lane >= 64, query, zero)], axis=0
        )
        near = pl.ds(part * half, span_keys)
        scores = lax.dot_general(
            query, keys[pair, near, :], (((1,), (1,)), ((), ())), preferred_element_type=F32
        )
        scores = jnp.concatenate(
            [jnp.where(low, scores[:, :lanes], -1e30), scores[:, lanes:edge]]
            + [
                jnp.where(keep, scores[:, edge + i * lanes : edge + (i + 1) * lanes], -1e30)
                for i, keep in enumerate(high)
            ],
            axis=1,
        )
        if with_max:
            scores = scores - jnp.max(scores, axis=1, keepdims=True)
            raised = jnp.exp2(scores)
            live = lax.dot_general(
                raised.astype(BF16), ones[near, :], (((1,), (0,)), ((), ())),
                preferred_element_type=F32,
            )
            weights = (raised / live[:, 0:1]).astype(BF16)
            both = dot(weights, values[pair, near, :])
        else:
            raised = jnp.exp2(scores).astype(BF16)
            both = dot(raised, jnp.concatenate([values[pair, near, :], ones[near, :]], axis=1))
            both = both[:, :lanes] / both[:, lanes:]
        attended[rows, span_of(pair * lanes, lanes, lanes)] = jnp.where(
            lane < 64, both[:half], both[half:]
        ).astype(BF16)

    def both_halves(with_max, pair, carry):
        for part in range(2):
            attend(pair, part, with_max)
        return carry

    @pl.when(small)
    def _():
        lax.fori_loop(0, pairs, functools.partial(both_halves, False), 0, unroll=4)

    @pl.when(jnp.logical_not(small))
    def _():
        lax.fori_loop(0, pairs, functools.partial(both_halves, True), 0)

    mixed[...] = (state[...].astype(F32) + dot(attended[...], out_weight[...])).astype(BF16)


VMEM = pl.BlockSpec(memory_space=pltpu.VMEM)
ANY = pl.BlockSpec(memory_space=pl.ANY)


def local(
    grid_rows,
    node_inputs,
    row_weight,
    node_weight,
    edge_bias,
    edge_out_weight,
    norm_gain,
    attn_weight,
    attn_out_weight,
    edge_source,
    edge_target,
    block_count,
):
    tile, width = node_inputs.shape
    rows = grid_rows.shape[0]
    hidden = row_weight.shape[1]
    blocks, edges = edge_source.shape
    regions, shards = lax.axis_size("region"), lax.axis_size("shard")
    pairs = width // 128
    dma = pltpu.SemaphoreType.DMA
    queries, keys, values, state, bounds, out_weight = pl.pallas_call(
        functools.partial(encode_kernel, regions, shards),
        out_shape=(
            pltpu.VMEM((pairs, tile, 128), BF16),
            pltpu.VMEM((pairs, KEYS, 128), BF16),
            pltpu.VMEM((pairs, KEYS, 128), BF16),
            pltpu.VMEM((tile, width), BF16),
            pltpu.VMEM((16, 128), F32),
            pltpu.VMEM((width, width), BF16),
        ),
        in_specs=[pl.BlockSpec(memory_space=pltpu.SMEM)] + [VMEM] * 4 + [ANY] * 7,
        out_specs=[VMEM] * 6,
        scratch_shapes=[
            pltpu.VMEM((rows, width), BF16),
            pltpu.VMEM(row_weight.shape, BF16),
            pltpu.VMEM(node_weight.shape, BF16),
            pltpu.VMEM(edge_out_weight.shape, BF16),
            pltpu.VMEM(attn_weight.shape, BF16),
            pltpu.VMEM((rows, hidden), BF16),
            pltpu.VMEM((rows + tile, hidden), BF16),
            pltpu.VMEM((blocks * edges, rows + tile), BF16),
            pltpu.VMEM((tile, blocks * edges), BF16),
            pltpu.VMEM((blocks * edges, hidden), BF16),
            pltpu.VMEM((KEYS, hidden), BF16),
            pltpu.VMEM((KEYS, width), BF16),
            dma((GRID_COPIES + 6,)),
            dma((regions - 1,)),
            dma((regions - 1,)),
            dma((len(SLOTS),)),
            dma((len(SLOTS),)),
            dma((len(SLOTS),)),
            dma((len(SLOTS),)),
        ],
        compiler_params=pltpu.CompilerParams(
            collective_id=0, has_side_effects=True, vmem_limit_bytes=55 * 2**20
        ),
        name="encode",
    )(
        block_count,
        edge_source,
        edge_target,
        edge_bias[None],
        norm_gain[None],
        grid_rows,
        node_inputs,
        row_weight,
        node_weight,
        edge_out_weight,
        attn_weight,
        attn_out_weight,
    )
    return pl.pallas_call(
        window_kernel,
        out_shape=jax.ShapeDtypeStruct((tile, width), BF16),
        in_specs=[VMEM] * 6,
        out_specs=VMEM,
        scratch_shapes=[
            pltpu.VMEM((tile, width), BF16),
            pltpu.VMEM((KEYS, 128), BF16),
        ],
        compiler_params=pltpu.CompilerParams(vmem_limit_bytes=24 * 2**20),
        name="window",
    )(bounds, queries, keys, values, state, out_weight)


def solution(mesh):
    placed = (
        P(("region", "shard"), None),
        P(("region", "shard"), None),
        P(),
        P(),
        P(),
        P(),
        P(),
        P(),
        P(),
        P(("region", "shard"), None),
        P(("region", "shard"), None),
        P(("region", "shard")),
    )
    return jax.shard_map(
        local, mesh=mesh, in_specs=placed, out_specs=P(("region", "shard"), None), check_vma=False
    )
```

```python
import functools

import jax
import jax.numpy as jnp
from jax import lax
from jax.experimental import pallas as pl
from jax.experimental.pallas import tpu as pltpu
from jax.sharding import PartitionSpec as P

HALF = 560
KEYS = 1408
OWN = 560
PLACES = {-1: (304, 256), 1: (816, 256), -2: (48, 256), 2: (1072, 256), -3: (0, 48), 3: (1328, 80)}
SLOTS = tuple(PLACES)
GRID_COPIES = 4
ACROSS = 4
LOG2E = 1.4426950408889634
F32 = jnp.float32
BF16 = jnp.bfloat16
MESH = pl.DeviceIdType.MESH


def dot(a, b):
    return jnp.dot(a, b, preferred_element_type=F32)


def span_of(start, size, unit):
    return pl.ds(pl.multiple_of(start, unit), size)


def encode_kernel(
    regions,
    shards,
    used,
    source,
    target,
    bias,
    gain,
    grid_hbm,
    nodes_hbm,
    row_hbm,
    node_hbm,
    edge_hbm,
    attn_hbm,
    out_hbm,
    queries,
    keys,
    values,
    state,
    bounds,
    out_weight,
    grid,
    row_weight,
    node_weight,
    edge_weight,
    attn_weight,
    projected,
    table,
    onehot,
    picks,
    hidden,
    sums,
    nodes,
    load_sem,
    row_send,
    row_recv,
    node_send,
    node_recv,
    sum_send,
    sum_recv,
):
    rows, width = grid.shape
    tile = state.shape[0]
    blocks, edges = source.shape
    part = rows // regions
    tiles = regions * shards
    region, shard = lax.axis_index("region"), lax.axis_index("shard")
    me = region * shards + shard

    def there(away):
        return (me + away >= 0) & (me + away < tiles)

    def device(away):
        return ((me + away) // shards, lax.rem(me + away, shards))

    def peer(step):
        return lax.rem(region + step, regions)

    loads = []
    piece = rows // GRID_COPIES

    def load(source_ref, target_ref):
        copy = pltpu.make_async_copy(source_ref, target_ref, load_sem.at[len(loads)])
        copy.start()
        loads.append(copy)
        return copy

    row_load = load(row_hbm, row_weight)
    grid_loads = [
        load(grid_hbm.at[pl.ds(i * piece, piece), :], grid.at[pl.ds(i * piece, piece), :])
        for i in range(GRID_COPIES)
    ]
    node_load = load(nodes_hbm, nodes.at[pl.ds(OWN, tile), :])
    node_weight_load = load(node_hbm, node_weight)
    edge_load = load(edge_hbm, edge_weight)
    attn_load = load(attn_hbm, attn_weight)
    out_load = load(out_hbm, out_weight)

    barrier = pltpu.get_barrier_semaphore()
    for step in range(1, regions):
        pl.semaphore_signal(barrier, inc=1, device_id=(peer(step), shard), device_id_type=MESH)
    for away in SLOTS:
        near = lax.rem(me + away + tiles, tiles)
        pl.semaphore_signal(
            barrier, inc=1, device_id=(near // shards, lax.rem(near, shards)), device_id_type=MESH
        )

    row_load.wait()
    for i in range(GRID_COPIES):
        grid_loads[i].wait()
        projected[pl.ds(i * piece, piece), :] = dot(
            grid[pl.ds(i * piece, piece), :], row_weight[...]
        ).astype(BF16)
    node_load.wait()

    pl.semaphore_wait(barrier, regions - 1 + len(SLOTS))

    here = span_of(region * part, part, part)
    row_copies = []
    for step in sorted(range(1, regions), key=lambda k: -min(k, regions - k)):
        copy = pltpu.make_async_remote_copy(
            projected.at[span_of(peer(step) * part, part, part), :],
            table.at[here, :],
            row_send.at[step - 1],
            row_recv.at[step - 1],
            device_id=(peer(step), shard),
            device_id_type=MESH,
        )
        copy.start()
        row_copies.append(copy)

    first_core = lax.rem(shard, 2) == 0
    partner = 1 - 2 * lax.rem(shard, 2)

    def halo(kind, slot, away, first):
        held, sends, receives = kind
        row, count = PLACES[slot]
        at = SLOTS.index(slot)
        return pltpu.make_async_remote_copy(
            held.at[pl.ds(first, count), :],
            held.at[pl.ds(row, count), :],
            sends.at[at],
            receives.at[at],
            device_id=device(away),
            device_id_type=MESH,
        )

    node_halo = (nodes, node_send, node_recv)
    sum_halo = (sums, sum_send, sum_recv)

    def first_copies(kind):
        return [
            (there(2), halo(kind, -2, 2, OWN)),
            (there(-2), halo(kind, 2, -2, OWN)),
            (first_core, halo(kind, -1, 1, OWN)),
            (jnp.logical_not(first_core), halo(kind, 1, -1, OWN)),
        ]

    def forwards(kind, came):
        if came < 0:
            return [
                (there(-2) & jnp.logical_not(first_core), halo(kind, -1, -1, PLACES[-2][0])),
                (there(-2) & there(1), halo(kind, -3, 1, PLACES[-2][0] + tile - PLACES[-3][1])),
            ]
        return [
            (there(2) & first_core, halo(kind, 1, 1, PLACES[2][0])),
            (there(2) & there(-1), halo(kind, 3, -1, PLACES[2][0])),
        ]

    def start(copies):
        for condition, copy in copies:
            pl.when(condition)(copy.start)

    start(first_copies(node_halo))

    table[here, :] = projected[here, :]
    node_weight_load.wait()
    table[pl.ds(rows, tile), :] = (
        dot(nodes[pl.ds(OWN, tile), :], node_weight[...]) + bias[...]
    ).astype(BF16)
    source_cols = jnp.transpose(source[...])
    target_cols = jnp.transpose(target[...])
    lane_rows = lax.broadcasted_iota(jnp.int32, (edges, rows), 1)
    lane_tile = lax.broadcasted_iota(jnp.int32, (edges, tile), 1)
    sub_tile = lax.broadcasted_iota(jnp.int32, (tile, edges), 0)
    limit = jnp.full((1, edges), used[0], jnp.int32)
    for block in range(blocks):
        span = pl.ds(block * edges, edges)
        onehot[span, pl.ds(0, rows)] = (
            (source_cols[:, block : block + 1] == lane_rows).astype(F32).astype(BF16)
        )
        onehot[span, pl.ds(rows, tile)] = (
            (target_cols[:, block : block + 1] == lane_tile).astype(F32).astype(BF16)
        )
        goal = jnp.where(limit > block, target[block : block + 1, :], -1)
        picks[:, span] = (goal == sub_tile).astype(F32).astype(BF16)

    for copy in row_copies:
        copy.wait()
    step_edges = 2 * edges
    for index in range(blocks * edges // step_edges):
        span = pl.ds(index * step_edges, step_edges)
        pre = dot(onehot[span, :], table[...])
        hidden[span, :] = (0.5 * pre * (1.0 + jnp.tanh(0.5 * pre))).astype(BF16)
    sums[pl.ds(OWN, tile), :] = dot(picks[...], hidden[...]).astype(BF16)
    start(first_copies(sum_halo))

    edge_load.wait()
    attn_load.wait()
    out_load.wait()

    def take(ref, spans):
        return jnp.concatenate([ref[span, :] for span in spans], axis=0)

    def normalised(spans):
        held = take(nodes, spans).astype(F32) + dot(take(sums, spans), edge_weight[...])
        held = held.astype(BF16)
        wide = held.astype(F32)
        centred = wide - jnp.mean(wide, axis=1, keepdims=True)
        spread = jnp.mean(centred * centred, axis=1, keepdims=True)
        return held, (centred * lax.rsqrt(spread + 1e-05) * gain[...]).astype(BF16)

    def project(normed, spans, flags):
        key = dot(normed, attn_weight[:, width : 2 * width])
        value = dot(normed, attn_weight[:, 2 * width :])
        begin = 0
        for span, flag in zip(spans, flags):
            rows_in = slice(begin, begin + span.size)
            begin += span.size
            for pair in range(width // 128):
                lanes = slice(pair * 128, pair * 128 + 128)
                keys[pair, span, :] = key[rows_in, lanes].astype(BF16)
                some = value[rows_in, lanes]
                values[pair, span, :] = (some if flag is None else some * flag).astype(BF16)
        return (
            jnp.max(key * key, axis=0, keepdims=True),
            jnp.max(jnp.abs(value), axis=0, keepdims=True),
        )

    own = pl.ds(OWN, tile)
    held, normed = normalised([own])
    state[...] = held
    query = dot(normed, attn_weight[:, :width]) * (LOG2E * 0.125)
    for pair in range(width // 128):
        queries[pair, :, :] = query[:, pair * 128 : pair * 128 + 128].astype(BF16)
    tops = project(normed, [own], [None])
    heads = (
        lax.broadcasted_iota(jnp.int32, (width, 128), 0) // 64
        == lax.broadcasted_iota(jnp.int32, (width, 128), 1)
    )
    heads = heads.astype(F32).astype(BF16)
    query_norm = jnp.max(dot((query * query).astype(BF16), heads), axis=0, keepdims=True)

    def arrive(slot):
        row, count = PLACES[slot]
        span = pl.ds(row, count)

        @pl.when(there(slot))
        def _():
            halo(node_halo, slot, 0, row).wait_recv()
            halo(sum_halo, slot, 0, row).wait_recv()

        @pl.when(jnp.logical_not(there(slot)))
        def _():
            nodes[span, :] = nodes[pl.ds(OWN, count), :]
            sums[span, :] = sums[pl.ds(OWN, count), :]

    def encode(spans, flags, tops):
        _, normed = normalised(spans)
        return tuple(jnp.maximum(a, b) for a, b in zip(tops, project(normed, spans, flags)))

    def choose(picks):
        row, flag = jnp.int32(0), F32(0)
        for condition, slot in picks:
            if abs(slot) == 1:
                pl.when(condition)(functools.partial(arrive, slot))
            row = jnp.where(condition, PLACES[slot][0], row)
            flag = jnp.where(condition, there(slot).astype(F32), flag)
        return [pl.ds(pl.multiple_of(row, 16), tile)], [flag]

    def far(slot):
        arrive(slot)
        for condition, copy in forwards(node_halo, slot) + forwards(sum_halo, slot):
            pl.when(condition)(copy.start)

    second_core = jnp.logical_not(first_core)
    tops = encode(*choose([(first_core, 1), (second_core, -1)]), tops)
    across, down = lax.rem(region, ACROSS), shard // 2
    late_low = (across == 0) & (down == 0)
    late_high = jnp.logical_not(late_low)
    crossing = late_low | ((across == ACROSS - 1) & (down == shards // 2 - 1))

    def far_late(condition):
        pl.when(condition & late_low)(functools.partial(far, -2))
        pl.when(condition & late_high)(functools.partial(far, 2))

    pl.when(late_low)(functools.partial(far, 2))
    pl.when(late_high)(functools.partial(far, -2))
    far_late(jnp.logical_not(crossing))
    row = jnp.where(late_low, PLACES[2][0], PLACES[-2][0])
    flag = jnp.where(late_low, there(2).astype(F32), there(-2).astype(F32))
    tops = encode([pl.ds(pl.multiple_of(row, 16), tile)], [flag], tops)
    early = late_low ^ first_core
    far_late(crossing & jnp.logical_not(early))
    tops = encode(
        *choose(
            [
                (early & first_core, -1),
                (early & second_core, 1),
                (jnp.logical_not(early) & late_low, -2),
                (jnp.logical_not(early) & late_high, 2),
            ]
        ),
        tops,
    )
    far_late(crossing & early)
    tops = encode(
        *choose(
            [
                (jnp.logical_not(early) & first_core, -1),
                (jnp.logical_not(early) & second_core, 1),
                (early & late_low, -2),
                (early & late_high, 2),
            ]
        ),
        tops,
    )
    last = [-3, 3]
    for slot in last:
        arrive(slot)
    tops = encode([pl.ds(*PLACES[slot]) for slot in last], [there(slot).astype(F32) for slot in last], tops)

    top_key, top_value = tops
    key_norm = dot(jnp.broadcast_to(top_key, (8, width)).astype(BF16), heads)
    bounds[0:8, :] = query_norm * key_norm
    bounds[8:16, :] = jnp.broadcast_to(jnp.max(top_value, axis=1, keepdims=True), (8, 128))
    for kind in (node_halo, sum_halo):
        for condition, copy in first_copies(kind) + forwards(kind, -2) + forwards(kind, 2):
            pl.when(condition)(copy.wait_send)


def window_kernel(
    bounds, queries, keys, values, state, out_weight, mixed,
    attended, ones,
):
    pairs, tile, lanes = queries.shape
    half = tile // 2
    span_keys = KEYS - half
    tiles = lax.axis_size("region") * lax.axis_size("shard")
    me = lax.axis_index("region") * lax.axis_size("shard") + lax.axis_index("shard")

    spot = lax.broadcasted_iota(jnp.int32, (KEYS, lanes), 0) - OWN + me * tile
    ones[...] = ((spot >= 0) & (spot < tiles * tile)).astype(F32).astype(BF16)
    lane = lax.broadcasted_iota(jnp.int32, (half, lanes), 1)
    row = lax.broadcasted_iota(jnp.int32, (2 * half, lanes), 0) % half
    key = lax.broadcasted_iota(jnp.int32, (2 * half, lanes), 1)
    low = key >= row
    edge = (2 * HALF) // lanes * lanes
    high = [key + at < row + 2 * HALF for at in range(edge, span_keys, lanes)]
    small = jnp.max(bounds[0:8, :]) < 6400.0
    small = small & (jnp.max(bounds[8:16, :]) < 1e9)

    def attend(pair, part, with_max):
        rows = slice(part * half, part * half + half)
        query = queries[pair, rows, :]
        zero = jnp.zeros_like(query)
        query = jnp.concatenate(
            [jnp.where(lane < 64, query, zero), jnp.where(lane >= 64, query, zero)], axis=0
        )
        near = pl.ds(part * half, span_keys)
        scores = lax.dot_general(
            query, keys[pair, near, :], (((1,), (1,)), ((), ())), preferred_element_type=F32
        )
        scores = jnp.concatenate(
            [jnp.where(low, scores[:, :lanes], -1e30), scores[:, lanes:edge]]
            + [
                jnp.where(keep, scores[:, edge + i * lanes : edge + (i + 1) * lanes], -1e30)
                for i, keep in enumerate(high)
            ],
            axis=1,
        )
        if with_max:
            scores = scores - jnp.max(scores, axis=1, keepdims=True)
            raised = jnp.exp2(scores)
            live = lax.dot_general(
                raised.astype(BF16), ones[near, :], (((1,), (0,)), ((), ())),
                preferred_element_type=F32,
            )
            weights = (raised / live[:, 0:1]).astype(BF16)
            both = dot(weights, values[pair, near, :])
        else:
            raised = jnp.exp2(scores).astype(BF16)
            both = dot(raised, jnp.concatenate([values[pair, near, :], ones[near, :]], axis=1))
            both = both[:, :lanes] / both[:, lanes:]
        attended[rows, span_of(pair * lanes, lanes, lanes)] = jnp.where(
            lane < 64, both[:half], both[half:]
        ).astype(BF16)

    def both_halves(with_max, pair, carry):
        for part in range(2):
            attend(pair, part, with_max)
        return carry

    @pl.when(small)
    def _():
        lax.fori_loop(0, pairs, functools.partial(both_halves, False), 0, unroll=8)

    @pl.when(jnp.logical_not(small))
    def _():
        lax.fori_loop(0, pairs, functools.partial(both_halves, True), 0)

    mixed[...] = (state[...].astype(F32) + dot(attended[...], out_weight[...])).astype(BF16)


VMEM = pl.BlockSpec(memory_space=pltpu.VMEM)
ANY = pl.BlockSpec(memory_space=pl.ANY)


def local(
    grid_rows,
    node_inputs,
    row_weight,
    node_weight,
    edge_bias,
    edge_out_weight,
    norm_gain,
    attn_weight,
    attn_out_weight,
    edge_source,
    edge_target,
    block_count,
):
    tile, width = node_inputs.shape
    rows = grid_rows.shape[0]
    hidden = row_weight.shape[1]
    blocks, edges = edge_source.shape
    regions, shards = lax.axis_size("region"), lax.axis_size("shard")
    pairs = width // 128
    dma = pltpu.SemaphoreType.DMA
    queries, keys, values, state, bounds, out_weight = pl.pallas_call(
        functools.partial(encode_kernel, regions, shards),
        out_shape=(
            pltpu.VMEM((pairs, tile, 128), BF16),
            pltpu.VMEM((pairs, KEYS, 128), BF16),
            pltpu.VMEM((pairs, KEYS, 128), BF16),
            pltpu.VMEM((tile, width), BF16),
            pltpu.VMEM((16, 128), F32),
            pltpu.VMEM((width, width), BF16),
        ),
        in_specs=[pl.BlockSpec(memory_space=pltpu.SMEM)] + [VMEM] * 4 + [ANY] * 7,
        out_specs=[VMEM] * 6,
        scratch_shapes=[
            pltpu.VMEM((rows, width), BF16),
            pltpu.VMEM(row_weight.shape, BF16),
            pltpu.VMEM(node_weight.shape, BF16),
            pltpu.VMEM(edge_out_weight.shape, BF16),
            pltpu.VMEM(attn_weight.shape, BF16),
            pltpu.VMEM((rows, hidden), BF16),
            pltpu.VMEM((rows + tile, hidden), BF16),
            pltpu.VMEM((blocks * edges, rows + tile), BF16),
            pltpu.VMEM((tile, blocks * edges), BF16),
            pltpu.VMEM((blocks * edges, hidden), BF16),
            pltpu.VMEM((KEYS, hidden), BF16),
            pltpu.VMEM((KEYS, width), BF16),
            dma((GRID_COPIES + 6,)),
            dma((regions - 1,)),
            dma((regions - 1,)),
            dma((len(SLOTS),)),
            dma((len(SLOTS),)),
            dma((len(SLOTS),)),
            dma((len(SLOTS),)),
        ],
        compiler_params=pltpu.CompilerParams(
            collective_id=0, has_side_effects=True, vmem_limit_bytes=55 * 2**20
        ),
        name="encode",
    )(
        block_count,
        edge_source,
        edge_target,
        edge_bias[None],
        norm_gain[None],
        grid_rows,
        node_inputs,
        row_weight,
        node_weight,
        edge_out_weight,
        attn_weight,
        attn_out_weight,
    )
    return pl.pallas_call(
        window_kernel,
        out_shape=jax.ShapeDtypeStruct((tile, width), BF16),
        in_specs=[VMEM] * 6,
        out_specs=VMEM,
        scratch_shapes=[
            pltpu.VMEM((tile, width), BF16),
            pltpu.VMEM((KEYS, 128), BF16),
        ],
        compiler_params=pltpu.CompilerParams(vmem_limit_bytes=24 * 2**20),
        name="window",
    )(bounds, queries, keys, values, state, out_weight)


def solution(mesh):
    placed = (
        P(("region", "shard"), None),
        P(("region", "shard"), None),
        P(),
        P(),
        P(),
        P(),
        P(),
        P(),
        P(),
        P(("region", "shard"), None),
        P(("region", "shard"), None),
        P(("region", "shard")),
    )
    return jax.shard_map(
        local, mesh=mesh, in_specs=placed, out_specs=P(("region", "shard"), None), check_vma=False
    )
```
